32 devices in a mesh: section: 2 (over core), tp: 4 (over y, x), pool: 4 (over z).
Axes of the slice: x: 2, y: 2, z: 4, core: 2. Of those that a mesh axis runs over, the one named last changes fastest.
Arguments:
- hidden: bfloat16 [2, 4, 128, 8192], P('section', 'pool', None, 'tp'), may hold values from -6 to 6
- queries: bfloat16 [2, 4, 16, 8, 64, 128], P('section', 'pool', None, None, 'tp'), may hold values from -450 to 450, as said below
- window_key_value: bfloat16 [2, 4, 16, 2, 8, 8, 128], P('section', 'pool', None, None, 'tp'), may hold values from -12 to 12
- cached_key_value: bfloat16 [2, 4, 128, 2, 8, 64, 128], P('section', 'pool', None, None, 'tp'), may hold values from -12 to 12
- cached_length: int32 [2, 4, 16], P('section', 'pool'), may hold values from 1 to 1024, 6144 in all within a row
- request_page_table: int32 [2, 4, 16, 16], P('section', 'pool'), may hold values from 0 to 127
- request_adapter: int32 [2, 4, 16], replicated, may hold values from 0 to 31, as said below
- layer_page_slot: int32 [64], replicated, may hold values from 0 to 63, as said below
- wo: bfloat16 [2, 8192, 8192], P('section', 'tp'), may hold values from -0.09375 to 0.09375
- adapter_down: bfloat16 [64, 64, 8192], P(('section', 'pool'), None, 'tp'), may hold values from -0.0625 to 0.0625
- adapter_up: bfloat16 [64, 64, 8192], P(('section', 'pool'), None, 'tp'), may hold values from -0.75 to 0.75
Outputs:
- next_hidden: bfloat16 [2, 4, 128, 8192], P('section', 'pool', None, 'tp')
The draws below stay inside these ranges and needn't reach their ends.
Inputs may be any that keep to these rules, and one draw needn't show every extreme that they name: `queries`: queries of order one; some entries far larger in the hidden draw. `request_page_table`: several requests may name the same cache page; entries past a request's length are read but excluded. `cached_length`: each request of a device has 1 to 1024 cached positions. `layer_page_slot`: the adapters of layer s occupy slots s * 32 to (s + 1) * 32 - 1, each slot once; slot q lies on the index q // 8 of section and pool taken together, section first, so layer s's pages sit on section s. `request_adapter`: up to all 16 requests of a pool group may use adapters held on one pool index, and one pool index may serve every request of its section.
All inputs are finite; a program needn't handle non-finite values.
Results may differ from the reference program's by a relative error of at most 0.009.
Values may be sent and summed in bfloat16 or wider, within the bound.
No kernel may reach another device: no remote copies, remote signals or barrier semaphores. Data moves between devices by JAX's collectives and lax.ppermute only.
A program may use at most 192 MiB of HBM per device.

```python
import math
import jax
import jax.numpy as jnp
import numpy as np
from jax import lax

MODEL_WIDTH = 8192
QUERY_HEADS = 64
KV_HEADS = 8
HEAD_WIDTH = 128
ADAPTER_RANK = 64
PAGE_TOK = 64
WINDOW_TOKENS = 8
GROUP_REQUESTS = 16
MAX_PAGES = 16
CACHE_PAGES = 128
PAGES_DEV = 8
ADAPTER_COUNT = 32
N_SECTION = 2
N_POOL = 4


def draw_queries(key, part):
    first_key = jax.random.fold_in(key, 11)
    array_shape = (N_SECTION, N_POOL, GROUP_REQUESTS, WINDOW_TOKENS, QUERY_HEADS, HEAD_WIDTH)
    values = jnp.clip(jax.random.normal(first_key, array_shape, jnp.float32), -5.0, 5.0)
    return values.astype(jnp.bfloat16)


def layer_shuffle(key):
    layer_key = jax.random.fold_in(key, 21)

    def one_layer(layer):
        return jax.random.permutation(jax.random.fold_in(layer_key, layer), ADAPTER_COUNT).astype(jnp.int32)
    layers = jnp.arange(N_SECTION, dtype=jnp.int32)
    return jax.vmap(one_layer)(layers)


def draw_layer_page_slot(key, part):
    shuffled = layer_shuffle(key)
    layers = jnp.arange(N_SECTION, dtype=jnp.int32)
    return (shuffled + layers[:, None] * ADAPTER_COUNT).reshape(N_SECTION * ADAPTER_COUNT).astype(jnp.int32)


def draw_request_adapter(key, part):
    shuffled = layer_shuffle(key)
    inverse = jnp.argsort(shuffled, axis=1, stable=True).astype(jnp.int32)
    base_key = jax.random.fold_in(key, 31)
    array_shape = (N_SECTION, N_POOL, GROUP_REQUESTS)
    busy_section = jax.random.randint(jax.random.fold_in(base_key, 1), (), 0, N_SECTION, jnp.int32)
    busy_owner = jax.random.randint(jax.random.fold_in(base_key, 2), (N_SECTION,), 0, N_POOL, jnp.int32)
    group_owner = jax.random.randint(jax.random.fold_in(base_key, 3), (N_SECTION, N_POOL), 0, N_POOL, jnp.int32)
    within = jax.random.randint(jax.random.fold_in(base_key, 4), array_shape, 0, PAGES_DEV, jnp.int32)
    first_pick = jax.random.randint(jax.random.fold_in(base_key, 5), array_shape, 0, ADAPTER_COUNT, jnp.int32)
    second_pick = jax.random.randint(jax.random.fold_in(base_key, 6), array_shape, 0, ADAPTER_COUNT, jnp.int32)
    rotation = jax.random.randint(jax.random.fold_in(base_key, 7), (N_SECTION, 1, 1), 0, ADAPTER_COUNT, jnp.int32)
    coin_flip = jax.random.randint(jax.random.fold_in(base_key, 8), array_shape, 0, 2, jnp.int32)
    spread_slot = (jnp.minimum(first_pick, second_pick) + rotation) % ADAPTER_COUNT
    owner_slot = group_owner[:, :, None] * PAGES_DEV + within
    busy_slot = busy_owner[:, None, None] * PAGES_DEV + within
    is_busy = (jnp.arange(N_SECTION, dtype=jnp.int32) == busy_section)[:, None, None]
    slot_local = jnp.where(is_busy, busy_slot, jnp.where(coin_flip == 1, owner_slot, spread_slot)).astype(jnp.int32)
    adapters = jnp.take_along_axis(inverse, slot_local.reshape(N_SECTION, N_POOL * GROUP_REQUESTS), axis=1)
    return adapters.reshape(array_shape).astype(jnp.int32)


def set_ends(entries, key, low, high):
    longest = entries.shape.index(max(entries.shape))
    spots = []
    for shift in (0, 1):
        where = [jax.random.randint(jax.random.fold_in(key, axis), (), 0, length) for axis, length in enumerate(entries.shape)]
        where[longest] = (where[longest] + shift) % entries.shape[longest]
        spots.append(tuple(where))
    return entries.at[spots[0]].set(low).at[spots[1]].set(high)


def spiked(drawn, rng, source, target, shards_of, factor):
    owner, partner = [(jnp.arange(drawn.shape[axis_at]) // (drawn.shape[axis_at] // shards_of)).reshape([-1 if axis == axis_at else 1 for axis in range(drawn.ndim)]) for axis_at in (source, target)]
    chosen = jax.random.permutation(rng, shards_of)[partner]
    strong = (owner == chosen) | (owner == (partner + shards_of // 2) % shards_of)
    return jnp.where(strong, factor * drawn, drawn)


def block_levels(own_key, shape, pieces, smallest, top_value):
    factor_of = 1.0
    for dim, parts in pieces:
        heights = jax.random.uniform(jax.random.fold_in(jax.random.fold_in(own_key, 6), dim), (parts,), jnp.float32, smallest / len(pieces), top_value / len(pieces))
        factor_of = factor_of * jnp.repeat(jnp.exp(heights), shape[dim] // parts).reshape((-1,) + (1,) * (len(shape) - 1 - dim))
    return factor_of


def length_profile(amount, total, most, skew):
    weights = [(1 << 20) // math.isqrt(standing ** skew) + 1 for standing in range(2, amount + 1)]
    rest, counts = total - most - (amount - 1), [1] * (amount - 1)
    while rest > 0:
        free = [i for i in range(amount - 1) if counts[i] < most]
        whole, left = sum([weights[i] for i in free]), rest
        for i in free:
            addition = min(most - counts[i], max(1, left * weights[i] // whole), rest)
            counts[i] = counts[i] + addition
            rest = rest - addition
    return np.array([most] + counts)


def ragged_sizes(rng, amount, total, reach, skew):
    if amount == 2:
        one = jax.random.randint(rng, (), max(1, total - reach), min(reach, total - 1) + 1)
        return jnp.stack([one, total - one])
    tallies = jnp.asarray(length_profile(amount, total, reach, skew), jnp.int32)
    couples = (amount - 1) // 2
    donor, sink = tallies[1:1 + 2 * couples:2], tallies[2:2 + 2 * couples:2]
    margin = jnp.minimum(donor - 1, reach - sink)
    moved = jax.random.randint(jax.random.fold_in(rng, 1), (couples,), 0, 1 << 20) % (margin + 1)
    tallies = tallies.at[1:1 + 2 * couples:2].set(donor - moved).at[2:2 + 2 * couples:2].set(sink + moved)
    return tallies[jax.random.permutation(jax.random.fold_in(rng, 2), amount)]


def scatter_about(own_key, dims, width, bound, shards=(), kind=jnp.bfloat16):
    array = jax.random.normal(own_key, dims, jnp.float32) * width
    if len(shards) > 0:
        array = block_levels(own_key, dims, shards, -0.22, 0.18) * array
    return jnp.clip(array, min=-bound, max=bound).astype(kind)


def bell_draw_with(key, extent, deviation, reach, shards, heavy, kind=jnp.bfloat16):
    array = deviation * jax.random.normal(key, extent, jnp.float32)
    if shards:
        array = array * block_levels(key, extent, shards, -0.22, 0.18)
    return jnp.clip(spiked(array, jax.random.fold_in(key, 3), *heavy), -reach, reach).astype(kind)


def setup_inputs(seed: int = 0) -> dict:
    key_list = jax.random.split(jax.random.key(seed), 12)
    hidden = scatter_about(key_list[0], (N_SECTION, N_POOL, GROUP_REQUESTS * WINDOW_TOKENS, MODEL_WIDTH), 1.0, 6.0, ((0, 2), (1, 4), (3, 4)))
    queries = draw_queries(jax.random.fold_in(key_list[11], 71), 0)
    window_key_value = scatter_about(key_list[2], (N_SECTION, N_POOL, GROUP_REQUESTS, 2, KV_HEADS, WINDOW_TOKENS, HEAD_WIDTH), 2.0, 12.0, ((0, 2), (1, 4), (4, 4)))
    cached_key_value = scatter_about(key_list[3], (N_SECTION, N_POOL, CACHE_PAGES, 2, KV_HEADS, PAGE_TOK, HEAD_WIDTH), 2.0, 12.0, ((0, 2), (1, 4), (4, 4)))
    cached_length = jax.vmap(lambda own: ragged_sizes(own, GROUP_REQUESTS, GROUP_REQUESTS * MAX_PAGES * PAGE_TOK * 3 // 8, MAX_PAGES * PAGE_TOK, 2))(jax.random.split(key_list[4], N_SECTION * N_POOL)).reshape((N_SECTION, N_POOL, GROUP_REQUESTS)).astype(jnp.int32)
    request_page_table = set_ends(jax.random.randint(key_list[5], (N_SECTION, N_POOL, GROUP_REQUESTS, MAX_PAGES), 0, CACHE_PAGES), jax.random.fold_in(key_list[5], 1), 0, CACHE_PAGES - 1).astype(jnp.int32)
    request_adapter = draw_request_adapter(jax.random.fold_in(key_list[11], 71), 0)
    layer_page_slot = draw_layer_page_slot(jax.random.fold_in(key_list[11], 71), 0)
    wo = bell_draw_with(key_list[8], (N_SECTION, QUERY_HEADS * HEAD_WIDTH, MODEL_WIDTH), (QUERY_HEADS * HEAD_WIDTH) ** -0.5, 0.09375, ((0, 2), (1, 4)), (1, 2, 4, 2.0))
    adapter_down = scatter_about(key_list[9], (N_SECTION * ADAPTER_COUNT, ADAPTER_RANK, QUERY_HEADS * HEAD_WIDTH), (QUERY_HEADS * HEAD_WIDTH) ** -0.5, 0.0625, ((0, 8), (2, 4)))
    adapter_up = scatter_about(key_list[10], (N_SECTION * ADAPTER_COUNT, ADAPTER_RANK, MODEL_WIDTH), ADAPTER_RANK ** -0.5, 0.75, ((0, 8), (2, 4)))
    return dict(hidden=hidden, queries=queries, window_key_value=window_key_value, cached_key_value=cached_key_value, cached_length=cached_length, request_page_table=request_page_table, request_adapter=request_adapter, layer_page_slot=layer_page_slot, wo=wo, adapter_down=adapter_down, adapter_up=adapter_up)


def attend(queries, cache_pages, window_kv, lengths, page_rows):
    requests, window, head_count, head_size = queries.shape
    kv_heads = window_kv.shape[2]
    page_tok = cache_pages.shape[3]
    max_pages = page_rows.shape[1]
    cached = max_pages * page_tok
    picked = jnp.take(cache_pages, page_rows, axis=0)
    picked = jnp.transpose(picked, (0, 2, 3, 1, 4, 5)).reshape(requests, 2, kv_heads, cached, head_size)
    keys_all = jnp.concatenate([picked, window_kv], axis=3).astype(jnp.float32)
    grouped = queries.reshape(requests, window, kv_heads, head_count // kv_heads, head_size).astype(jnp.float32)
    scores = jnp.einsum("rwkgd,rktd->rkgwt", grouped, keys_all[:, 0], precision=lax.Precision.HIGHEST) * (head_size ** -0.5)
    position = jnp.arange(cached + window, dtype=jnp.int32)
    query_pos = jnp.arange(window, dtype=jnp.int32)
    in_cache = position[None, :] < lengths[:, None]
    in_window = (position[None, :] >= cached) & (position[None, :] - cached <= query_pos[:, None])
    allowed = in_cache[:, None, :] | in_window[None, :, :]
    scores = jnp.where(allowed[:, None, None, :, :], scores, -jnp.inf)
    largest = jnp.max(scores, axis=-1, keepdims=True)
    weights = jnp.exp(scores - largest)
    probs = (weights / jnp.sum(weights, axis=-1, keepdims=True)).astype(jnp.bfloat16)
    context = jnp.einsum("rkgwt,rktd->rwkgd", probs.astype(jnp.float32), keys_all[:, 1], precision=lax.Precision.HIGHEST)
    return context.reshape(requests, window, head_count * head_size).astype(jnp.bfloat16)


def reference(hidden, queries, window_key_value, cached_key_value, cached_length, request_page_table, request_adapter, layer_page_slot, wo, adapter_down, adapter_up):
    def one_group(group_id):
        section_index = group_id // N_POOL
        pool_index = group_id % N_POOL
        context = attend(queries[section_index, pool_index], cached_key_value[section_index, pool_index], window_key_value[section_index, pool_index], cached_length[section_index, pool_index], request_page_table[section_index, pool_index])
        flat_rows = context.reshape(GROUP_REQUESTS * WINDOW_TOKENS, QUERY_HEADS * HEAD_WIDTH)
        plain_output = jnp.dot(flat_rows, wo[section_index], preferred_element_type=jnp.float32)
        slot_indices = layer_page_slot[section_index * ADAPTER_COUNT + request_adapter[section_index, pool_index]].astype(jnp.int32)
        chosen_down = jnp.take(adapter_down, slot_indices, axis=0).astype(jnp.float32)
        chosen_up = jnp.take(adapter_up, slot_indices, axis=0).astype(jnp.float32)
        rank_hidden = jnp.einsum("rwh,rkh->rwk", context.astype(jnp.float32), chosen_down, precision=lax.Precision.HIGHEST).astype(jnp.bfloat16)
        adapter_delta = jnp.einsum("tol,tlh->toh", rank_hidden.astype(jnp.float32), chosen_up, precision=lax.Precision.HIGHEST).astype(jnp.bfloat16)
        adapter_delta = adapter_delta.reshape(GROUP_REQUESTS * WINDOW_TOKENS, MODEL_WIDTH).astype(jnp.float32)
        blended_output = hidden[section_index, pool_index].astype(jnp.float32) + plain_output + adapter_delta
        return blended_output.astype(jnp.bfloat16)

    results = lax.map(one_group, jnp.arange(N_SECTION * N_POOL, dtype=jnp.int32))
    results = results.reshape(N_SECTION, N_POOL, GROUP_REQUESTS * WINDOW_TOKENS, MODEL_WIDTH)
    return jnp.roll(results, 1, axis=0)
```

```python
import functools
import math

import jax
import jax.numpy as jnp
from jax import lax
from jax.experimental import pallas as pl
from jax.experimental.pallas import tpu as pltpu
from jax.sharding import PartitionSpec as P


CHUNKS = 2
KEY_BLOCK = 512
ITEMS = 2


def attend_kernel(first, lengths, pages, queries, window, cache, out, keys, sems, item_request, item_block, ordered, tops, sums, parts, wide, near_scores, far_scores, near_probs, far_probs):
    requests, rows_all, head_size = ordered.shape
    kv_heads = keys.shape[2]
    page_tok = cache.shape[3]
    window_len = window.shape[3]
    key_block = min(KEY_BLOCK, keys.shape[3])
    blocks = keys.shape[3] // key_block
    per_block = key_block // page_tok
    rows = rows_all // kv_heads
    heads_all = rows_all // window_len
    factor = head_size ** (-0.5) * math.log2(math.e)

    def page_copy(r, j):
        return pltpu.make_async_copy(
            cache.at[pages[first + r, j]],
            keys.at[r, :, :, pl.ds(pl.multiple_of(j * page_tok, page_tok), page_tok), :],
            sems.at[r, j],
        )

    def used_pages(r):
        return (lengths[first + r] + page_tok - 1) // page_tok

    def used_blocks(r):
        return (lengths[first + r] + key_block - 1) // key_block

    def start_request(r, items):
        count = used_pages(r)

        def one(j, c):
            page_copy(r, j).start()
            return c

        lax.fori_loop(0, count, one, 0)

        def clear(j, c):
            at = pl.ds(pl.multiple_of(j * page_tok, page_tok), page_tok)
            keys[r, 1, :, at, :] = jnp.zeros((kv_heads, page_tok, head_size), keys.dtype)
            return c

        lax.fori_loop(count, used_blocks(r) * per_block, clear, 0)

        def note(b, at):
            item_request[at] = r
            item_block[at] = b
            return at + 1

        return lax.fori_loop(0, used_blocks(r), note, items)

    items = lax.fori_loop(0, requests, start_request, 0)
    item_request[items] = 0
    item_block[items] = 0

    target = lax.broadcasted_iota(jnp.int32, (rows_all, rows_all), 0)
    source = lax.broadcasted_iota(jnp.int32, (rows_all, rows_all), 1)
    moved = (target % window_len) * heads_all + target // window_len
    permutation = jnp.where(source == moved, 1.0, 0.0).astype(jnp.bfloat16)

    def prepare(r, carry):
        ordered[r] = jnp.dot(
            permutation, queries[r], preferred_element_type=jnp.float32
        ).astype(jnp.bfloat16)
        return carry

    lax.fori_loop(0, requests, prepare, 0, unroll=4)

    last = (((1,), (1,)), ((), ()))
    win_cols = requests * window_len
    win_col = lax.broadcasted_iota(jnp.int32, (rows, win_cols), 1)
    win_row = lax.broadcasted_iota(jnp.int32, (rows, win_cols), 0)
    win_of = jnp.where((win_col % window_len) <= (win_row % window_len), win_col // window_len, -1)
    col = lax.broadcasted_iota(jnp.int32, (rows, key_block), 1)
    win_keys = []
    win_values = []
    for k in range(kv_heads):
        for store, kind in ((win_keys, 0), (win_values, 1)):
            taken = window[:, kind, k].astype(jnp.float32).reshape(win_cols, head_size)
            store.append(taken.astype(jnp.bfloat16))

    def item_step(i, carry):
        work = []
        for u in range(ITEMS):
            at = jnp.minimum(i * ITEMS + u, items)
            real = at < items
            r, b = item_request[at], item_block[at]
            stop = jnp.where(real, jnp.minimum(used_pages(r), (b + 1) * per_block), 0)

            def arrive(j, c, r=r):
                page_copy(r, j).wait()
                return c

            lax.fori_loop(b * per_block, stop, arrive, 0)
            work.append((r, b, jnp.where(real, r * blocks + b, requests * blocks)))
        chains = [(u, k) for u in range(ITEMS) for k in range(kv_heads)]
        peaks = {}
        for u, k in chains:
            r, b, slot = work[u]
            span = pl.ds(pl.multiple_of(b * key_block, key_block), key_block)
            asked = ordered[r, k * rows : (k + 1) * rows, :]
            near = lax.dot_general(asked, win_keys[k], last, preferred_element_type=jnp.float32)
            far = lax.dot_general(
                asked, keys[r, 0, k, span, :], last, preferred_element_type=jnp.float32
            )
            near = jnp.where(win_of == jnp.where(b == 0, r, requests), near, -jnp.inf)
            far = jnp.where(col < lengths[first + r] - b * key_block, far, -jnp.inf)
            near_scores[u, k] = near
            far_scores[u, k] = far
            peaks[u, k] = jnp.maximum(
                jnp.max(near, axis=-1, keepdims=True), jnp.max(far, axis=-1, keepdims=True)
            )
        for u, k in chains:
            slot = work[u][2]
            top = peaks[u, k]
            near = jnp.exp2((near_scores[u, k] - top) * factor)
            far = jnp.exp2((far_scores[u, k] - top) * factor)
            near_probs[u, k] = near.astype(jnp.bfloat16)
            far_probs[u, k] = far.astype(jnp.bfloat16)
            total = jnp.sum(near, axis=-1, keepdims=True) + jnp.sum(far, axis=-1, keepdims=True)
            tops[slot, k] = jnp.broadcast_to(top, (rows, head_size))
            sums[slot, k] = jnp.broadcast_to(total, (rows, head_size))
        for u, k in chains:
            r, b, slot = work[u]
            span = pl.ds(pl.multiple_of(b * key_block, key_block), key_block)
            parts[slot, k] = jnp.dot(
                far_probs[u, k], keys[r, 1, k, span, :], preferred_element_type=jnp.float32
            ) + jnp.dot(near_probs[u, k], win_values[k], preferred_element_type=jnp.float32)
        return carry

    lax.fori_loop(0, (items + ITEMS - 1) // ITEMS, item_step, 0)

    def combine(r, carry):
        count = used_blocks(r)
        at = pl.ds(pl.multiple_of(r * window_len, window_len), window_len)
        for k in range(kv_heads):
            top = tops[r * blocks, k]
            for b in range(1, blocks):
                top = jnp.where(b < count, jnp.maximum(top, tops[r * blocks + b, k]), top)
            total, value = 0.0, 0.0
            for b in range(blocks):
                share = jnp.exp2((tops[r * blocks + b, k] - top) * factor)
                added = sums[r * blocks + b, k] * share
                moved = parts[r * blocks + b, k] * share
                total = total + (added if b == 0 else jnp.where(b < count, added, 0.0))
                value = value + (moved if b == 0 else jnp.where(b < count, moved, 0.0))
            value = value / total
            for g in range(rows // window_len):
                start = (k * (rows // window_len) + g) * head_size
                wide[at, start : start + head_size] = value[g * window_len : (g + 1) * window_len]
        return carry

    lax.fori_loop(0, requests, combine, 0, unroll=2)
    out[...] = wide[...].astype(out.dtype)


def attend(first, requests, queries, window, cache, lengths, pages):
    _, window_len, heads, head_size = queries.shape
    kv_heads, page_tok = cache.shape[2], cache.shape[3]
    max_keys = pages.shape[1] * page_tok
    rows_all = window_len * heads
    rows = rows_all // kv_heads
    slots = requests * (max_keys // min(KEY_BLOCK, max_keys)) + 1
    flat = queries.reshape(queries.shape[0], rows_all, head_size)
    smem = pl.BlockSpec(memory_space=pltpu.SMEM)
    take = first // requests
    return pl.pallas_call(
        functools.partial(attend_kernel, first),
        grid=(1,),
        in_specs=[
            smem,
            smem,
            pl.BlockSpec((requests, rows_all, head_size), lambda i: (take, 0, 0)),
            pl.BlockSpec((requests,) + window.shape[1:], lambda i: (take, 0, 0, 0, 0)),
            pl.BlockSpec(memory_space=pl.ANY),
        ],
        out_specs=pl.BlockSpec((requests * window_len, heads * head_size), lambda i: (0, 0)),
        out_shape=jax.ShapeDtypeStruct((requests * window_len, heads * head_size), jnp.bfloat16),
        scratch_shapes=[
            pltpu.VMEM((requests, 2, kv_heads, max_keys, head_size), jnp.bfloat16),
            pltpu.SemaphoreType.DMA((requests, pages.shape[1])),
            pltpu.SMEM((slots + 1,), jnp.int32),
            pltpu.SMEM((slots + 1,), jnp.int32),
            pltpu.VMEM((requests, rows_all, head_size), jnp.bfloat16),
            pltpu.VMEM((slots, kv_heads, rows, head_size), jnp.float32),
            pltpu.VMEM((slots, kv_heads, rows, head_size), jnp.float32),
            pltpu.VMEM((slots, kv_heads, rows, head_size), jnp.float32),
            pltpu.VMEM((requests * window_len, heads * head_size), jnp.float32),
            pltpu.VMEM((ITEMS, kv_heads, rows, requests * window_len), jnp.float32),
            pltpu.VMEM((ITEMS, kv_heads, rows, min(KEY_BLOCK, max_keys)), jnp.float32),
            pltpu.VMEM((ITEMS, kv_heads, rows, requests * window_len), jnp.bfloat16),
            pltpu.VMEM((ITEMS, kv_heads, rows, min(KEY_BLOCK, max_keys)), jnp.bfloat16),
        ],
        cost_estimate=pl.CostEstimate(flops=500000000, bytes_accessed=12000000, transcendentals=0),
        name="attend",
    )(lengths, pages, flat, window, cache)


def project_kernel(piece, *refs):
    count = len(refs) - 5
    rows, weights, out = refs[:count], refs[count], refs[count + 1]
    held, stored, sems = refs[count + 2 :]
    blocks, _, block = stored.shape
    each = held.shape[0] // count
    start = piece[0] * (blocks * block)

    def row_copy(i):
        return pltpu.make_async_copy(
            rows[i], held.at[pl.ds(i * each, each)], sems.at[blocks + i]
        )

    def weight_copy(b):
        at = pl.ds(pl.multiple_of(start + b * block, block), block)
        return pltpu.make_async_copy(weights.at[:, at], stored.at[b], sems.at[b])

    for i in range(count):
        row_copy(i).start()
    for b in range(blocks):
        weight_copy(b).start()
    for i in range(count):
        row_copy(i).wait()

    def step(b, carry):
        weight_copy(b).wait()
        at = pl.ds(pl.multiple_of(b * block, block), block)
        out[:, at] = jnp.dot(
            held[...], stored[b], preferred_element_type=jnp.float32
        ).astype(out.dtype)
        return carry

    lax.fori_loop(0, blocks, step, 0)


def project(chunks, weights, piece, pieces):
    depth, width = weights.shape
    own = width // pieces
    block = min(256, own)
    blocks = own // block
    total = sum(c.shape[0] for c in chunks)
    anywhere = pl.BlockSpec(memory_space=pl.ANY)
    return pl.pallas_call(
        project_kernel,
        in_specs=[pl.BlockSpec(memory_space=pltpu.SMEM)] + [anywhere] * (len(chunks) + 1),
        out_specs=pl.BlockSpec(memory_space=pltpu.VMEM),
        out_shape=jax.ShapeDtypeStruct((total, own), jnp.bfloat16),
        scratch_shapes=[
            pltpu.VMEM((total, depth), jnp.bfloat16),
            pltpu.VMEM((blocks, depth, block), jnp.bfloat16),
            pltpu.SemaphoreType.DMA((blocks + len(chunks),)),
        ],
        cost_estimate=pl.CostEstimate(
            flops=2 * total * depth * own,
            bytes_accessed=2 * (depth * own + total * (depth + own)),
            transcendentals=0,
        ),
        name="project",
    )(jnp.reshape(piece, (1,)).astype(jnp.int32), *chunks, weights)


def pick(table, index):
    value = jnp.int32(table[0])
    for i in range(1, len(table)):
        value = jnp.where(index == i, jnp.int32(table[i]), value)
    return value


def local_slots(where, adapters_of, slot_of, order, steps, first, count, pages_here):
    section, pool = where[0], where[1]
    adapters = slot_of.shape[0] // adapters_of.shape[0]
    place_of = [order.index(p) for p in range(len(order))]
    place = pick(place_of, pool)
    slots = []
    for step in steps:
        group = pick(order, lax.rem(place - step + len(order), len(order)))
        for r in range(count):
            slot = slot_of[section * adapters + adapters_of[section, group, first + r]]
            slots.append(slot - section * adapters - pool * pages_here)
    return slots


def rank_kernel(order, steps, first, count, where, adapters_of, slot_of, down, *refs):
    held, out = refs[:-1], refs[-1]
    pages_here, rank_width, features = down.shape
    wide_cols = pages_here * rank_width
    lanes = out.shape[1]
    slots = local_slots(where, adapters_of, slot_of, order, steps, first, count, pages_here)
    rows = jnp.concatenate([h[...] for h in held], axis=0)
    wide = lax.dot_general(
        rows, down[...].reshape(wide_cols, features), (((1,), (1,)), ((), ())),
        preferred_element_type=jnp.float32,
    )
    window_len = rows.shape[0] // len(slots)
    page = lax.broadcasted_iota(jnp.int32, (window_len, wide_cols), 1) // rank_width
    folded = []
    for i, slot in enumerate(slots):
        kept = jnp.where(page == slot, wide[i * window_len : (i + 1) * window_len], 0.0)
        total = kept[:, :lanes]
        for start in range(lanes, wide_cols, lanes):
            total = total + kept[:, start : start + lanes]
        folded.append(total)
    out[...] = jnp.concatenate(folded, axis=0).astype(out.dtype)


def up_kernel(order, first, count, parts, where, adapters_of, slot_of, up, *refs):
    ranks, outs = refs[:parts], refs[parts:]
    pages_here, rank_width, features = up.shape
    wide_cols = pages_here * rank_width
    lanes = ranks[0].shape[1]
    steps = range(len(order))
    slots = local_slots(where, adapters_of, slot_of, order, steps, first, count, pages_here)
    total = ranks[0][...].astype(jnp.float32)
    for other in ranks[1:]:
        total = total + other[...].astype(jnp.float32)
    window_len = total.shape[0] // len(slots)
    page = lax.broadcasted_iota(jnp.int32, (window_len, wide_cols), 1) // rank_width
    spread = []
    for i, slot in enumerate(slots):
        block = total[i * window_len : (i + 1) * window_len]
        tiled = jnp.concatenate([block] * (wide_cols // lanes), axis=1)
        spread.append(jnp.where(page == slot, tiled, 0.0))
    spread = jnp.concatenate(spread, axis=0).astype(jnp.bfloat16)
    weights = up[...].reshape(wide_cols, features)
    each = outs[0].shape[0]
    block = min(512, features)
    for start in range(0, features, block):
        made = jnp.dot(
            spread, weights[:, start : start + block], preferred_element_type=jnp.float32
        ).astype(jnp.bfloat16)
        for i, out in enumerate(outs):
            out[:, start : start + block] = made[i * each : (i + 1) * each]


def small_call(kernel, where, adapters_of, slot_of, weights, arrays, outs, flops):
    smem = pl.BlockSpec(memory_space=pltpu.SMEM)

    def whole(x):
        return pl.BlockSpec(x.shape, lambda i: (0,) * len(x.shape))

    moved = weights.size + sum(x.size for x in arrays)
    return pl.pallas_call(
        kernel,
        grid=(1,),
        in_specs=[smem] * 3 + [whole(weights)] + [whole(x) for x in arrays],
        out_specs=[whole(x) for x in outs],
        out_shape=outs,
        cost_estimate=pl.CostEstimate(flops=flops, bytes_accessed=2 * moved, transcendentals=0),
    )(where, adapters_of, slot_of, weights, *arrays)


def after(value, *earlier):
    return lax.optimization_barrier((value,) + earlier)[0]


def per_device(
    hidden,
    queries,
    window_key_value,
    cached_key_value,
    cached_length,
    request_page_table,
    request_adapter,
    layer_page_slot,
    wo,
    adapter_down,
    adapter_up,
):
    sections = lax.axis_size("section")
    pools = lax.axis_size("pool")
    splits = lax.axis_size("tp")
    section = lax.axis_index("section")
    pool = lax.axis_index("pool")
    split = lax.axis_index("tp")
    groups = queries.shape[2]
    window_len = queries.shape[3]
    part = groups // CHUNKS
    part_rows = part * window_len
    pages_here, rank_width, features = adapter_down.shape
    own_width = adapter_up.shape[2]
    wide_cols = pages_here * rank_width

    order = list(range(0, pools, 2)) + list(range(1, pools, 2))[::-1]
    ring = [(order[i], order[(i + 1) % pools]) for i in range(pools)]
    ring_next = [
        (s * pools + a, ((s + 1) % sections) * pools + b) for s in range(sections) for a, b in ring
    ]
    forward = [(s, (s + 1) % sections) for s in range(sections)]
    where = jnp.stack([section, pool]).astype(jnp.int32)

    def attend_part(c, asked):
        return attend(
            c * part,
            part,
            asked,
            window_key_value[0, 0],
            cached_key_value[0, 0],
            cached_length[0, 0],
            request_page_table[0, 0],
        )

    def gather(value):
        return lax.ppermute(value, "pool", ring)

    offsets = list(range(splits - 1, 0, -1)) + [0]

    def project_piece(i, *earlier):
        d = offsets[i]
        first = after(contexts[0], *earlier)
        piece = project([first] + contexts[1:], wo[0], split ^ d, splits)
        pairs = [
            (s * splits + t, ((s + 1) % sections) * splits + (t ^ d))
            for s in range(sections)
            for t in range(splits)
        ]
        arrived.append(lax.ppermute(piece, ("section", "tp"), pairs))
        return piece

    lanes = min(128, wide_cols)

    def rank_of(c, earlier):
        arrays = [after(held[c][0], earlier)] + held[c][1:]
        return small_call(
            functools.partial(rank_kernel, order, list(range(pools)), c * part, part),
            where,
            request_adapter,
            layer_page_slot,
            adapter_down,
            arrays,
            [jax.ShapeDtypeStruct((pools * part_rows, lanes), jnp.bfloat16)],
            2 * pools * part_rows * wide_cols * features,
        )[0]

    def up_of(c, mine, earlier):
        ranks = [after(mine, earlier)]
        for d in range(splits - 1, 0, -1):
            pairs = [(t, t ^ d) for t in range(splits)]
            ranks.append(lax.ppermute(mine, "tp", pairs))
        outs = small_call(
            functools.partial(up_kernel, order, c * part, part, len(ranks)),
            where,
            request_adapter,
            layer_page_slot,
            adapter_up,
            ranks,
            [jax.ShapeDtypeStruct((part_rows, own_width), jnp.bfloat16)] * pools,
            2 * pools * part_rows * wide_cols * own_width,
        )
        return outs

    def scatter(step, value):
        if step == pools - 1:
            return lax.ppermute(value, ("section", "pool"), ring_next)
        return lax.ppermute(value, "pool", ring)

    hidden_in = lax.ppermute(hidden[0, 0], "section", forward)
    arrived = []
    contexts = [attend_part(0, queries[0, 0])]
    contexts.append(attend_part(1, after(queries[0, 0], contexts[0])))
    held = [[c] for c in contexts]
    held[0].append(gather(contexts[0]))
    held[0].append(gather(held[0][1]))
    held[1].append(gather(contexts[1]))
    piece = project_piece(0, held[0][1])
    held[0].append(gather(after(held[0][2], piece)))
    piece = project_piece(1, piece, held[0][2])
    held[1].append(gather(after(held[1][1], piece)))
    piece = project_piece(2, piece, held[1][1])
    for _ in range(4, pools):
        held[0].append(gather(held[0][-1]))
    rank0 = rank_of(0, piece)
    held[1].append(gather(after(held[1][2], rank0)))
    for _ in range(4, pools):
        held[1].append(gather(held[1][-1]))
    outs0 = up_of(0, rank0, held[1][2])
    own0 = lax.ppermute(outs0[0], "section", forward)
    moving0 = scatter(1, outs0[1])
    rank1 = rank_of(1, outs0[0])
    moving0 = scatter(2, after(moving0, rank1) + outs0[2])
    outs1 = up_of(1, rank1, rank1)
    own1 = lax.ppermute(outs1[0], "section", forward)
    moving1 = scatter(1, outs1[1])
    piece = project_piece(3, piece, outs1[0])
    moving0 = scatter(3, after(moving0, piece) + outs0[3])
    moving1 = scatter(2, after(moving1, piece) + outs1[2])
    moving1 = scatter(3, moving1 + outs1[3])
    for step in range(4, pools):
        moving0 = scatter(step, moving0 + outs0[step])
        moving1 = scatter(step, moving1 + outs1[step])

    base = hidden_in.astype(jnp.float32)
    for piece in arrived:
        base = base + piece.astype(jnp.float32)
    delta = jnp.concatenate(
        [
            own0.astype(jnp.float32) + moving0.astype(jnp.float32),
            own1.astype(jnp.float32) + moving1.astype(jnp.float32),
        ]
    )
    return (base + delta).astype(jnp.bfloat16)[None, None]


def solution(mesh):
    return jax.shard_map(
        per_device,
        mesh=mesh,
        in_specs=(
            P("section", "pool", None, "tp"),
            P("section", "pool", None, None, "tp", None),
            P("section", "pool", None, None, "tp", None, None),
            P("section", "pool", None, None, "tp", None, None),
            P("section", "pool", None),
            P("section", "pool", None, None),
            P(),
            P(),
            P("section", "tp", None),
            P(("section", "pool"), None, "tp"),
            P(("section", "pool"), None, "tp"),
        ),
        out_specs=P("section", "pool", None, "tp"),
        check_vma=False,
    )
```

```python
import functools
import math

import jax
import jax.numpy as jnp
from jax import lax
from jax.experimental import pallas as pl
from jax.experimental.pallas import tpu as pltpu
from jax.sharding import PartitionSpec as P


CHUNKS = 2
KEY_BLOCK = 512
ITEMS = 2


def attend_kernel(first, lengths, pages, queries, window, cache, out, keys, sems, item_request, item_block, ordered, tops, sums, parts, wide, near_scores, far_scores, near_probs, far_probs):
    requests, rows_all, head_size = ordered.shape
    kv_heads = keys.shape[2]
    page_tok = cache.shape[3]
    window_len = window.shape[3]
    key_block = min(KEY_BLOCK, keys.shape[3])
    blocks = keys.shape[3] // key_block
    per_block = key_block // page_tok
    rows = rows_all // kv_heads
    heads_all = rows_all // window_len
    factor = head_size ** (-0.5) * math.log2(math.e)

    def page_copy(r, j):
        return pltpu.make_async_copy(
            cache.at[pages[first + r, j]],
            keys.at[r, :, :, pl.ds(pl.multiple_of(j * page_tok, page_tok), page_tok), :],
            sems.at[r, j],
        )

    def used_pages(r):
        return (lengths[first + r] + page_tok - 1) // page_tok

    def used_blocks(r):
        return (lengths[first + r] + key_block - 1) // key_block

    def start_request(r, items):
        count = used_pages(r)

        def one(j, c):
            page_copy(r, j).start()
            return c

        lax.fori_loop(0, count, one, 0)

        def clear(j, c):
            at = pl.ds(pl.multiple_of(j * page_tok, page_tok), page_tok)
            keys[r, 1, :, at, :] = jnp.zeros((kv_heads, page_tok, head_size), keys.dtype)
            return c

        lax.fori_loop(count, used_blocks(r) * per_block, clear, 0)

        def note(b, at):
            item_request[at] = r
            item_block[at] = b
            return at + 1

        return lax.fori_loop(0, used_blocks(r), note, items)

    items = lax.fori_loop(0, requests, start_request, 0)
    item_request[items] = 0
    item_block[items] = 0

    target = lax.broadcasted_iota(jnp.int32, (rows_all, rows_all), 0)
    source = lax.broadcasted_iota(jnp.int32, (rows_all, rows_all), 1)
    moved = (target % window_len) * heads_all + target // window_len
    permutation = jnp.where(source == moved, 1.0, 0.0).astype(jnp.bfloat16)

    def prepare(r, carry):
        ordered[r] = jnp.dot(
            permutation, queries[r], preferred_element_type=jnp.float32
        ).astype(jnp.bfloat16)
        return carry

    lax.fori_loop(0, requests, prepare, 0, unroll=4)

    last = (((1,), (1,)), ((), ()))
    win_cols = requests * window_len
    win_col = lax.broadcasted_iota(jnp.int32, (rows, win_cols), 1)
    win_row = lax.broadcasted_iota(jnp.int32, (rows, win_cols), 0)
    win_of = jnp.where((win_col % window_len) <= (win_row % window_len), win_col // window_len, -1)
    col = lax.broadcasted_iota(jnp.int32, (rows, key_block), 1)
    win_keys = []
    win_values = []
    for k in range(kv_heads):
        for store, kind in ((win_keys, 0), (win_values, 1)):
            taken = window[:, kind, k].astype(jnp.float32).reshape(win_cols, head_size)
            store.append(taken.astype(jnp.bfloat16))

    def item_step(i, carry):
        work = []
        for u in range(ITEMS):
            at = jnp.minimum(i * ITEMS + u, items)
            real = at < items
            r, b = item_request[at], item_block[at]
            stop = jnp.where(real, jnp.minimum(used_pages(r), (b + 1) * per_block), 0)

            def arrive(j, c, r=r):
                page_copy(r, j).wait()
                return c

            lax.fori_loop(b * per_block, stop, arrive, 0)
            work.append((r, b, jnp.where(real, r * blocks + b, requests * blocks)))
        chains = [(u, k) for u in range(ITEMS) for k in range(kv_heads)]
        peaks = {}
        for u, k in chains:
            r, b, slot = work[u]
            span = pl.ds(pl.multiple_of(b * key_block, key_block), key_block)
            asked = ordered[r, k * rows : (k + 1) * rows, :]
            near = lax.dot_general(asked, win_keys[k], last, preferred_element_type=jnp.float32)
            far = lax.dot_general(
                asked, keys[r, 0, k, span, :], last, preferred_element_type=jnp.float32
            )
            near = jnp.where(win_of == jnp.where(b == 0, r, requests), near, -jnp.inf)
            far = jnp.where(col < lengths[first + r] - b * key_block, far, -jnp.inf)
            near_scores[u, k] = near
            far_scores[u, k] = far
            peaks[u, k] = jnp.maximum(
                jnp.max(near, axis=-1, keepdims=True), jnp.max(far, axis=-1, keepdims=True)
            )
        for u, k in chains:
            slot = work[u][2]
            top = peaks[u, k]
            near = jnp.exp2((near_scores[u, k] - top) * factor)
            far = jnp.exp2((far_scores[u, k] - top) * factor)
            near_probs[u, k] = near.astype(jnp.bfloat16)
            far_probs[u, k] = far.astype(jnp.bfloat16)
            total = jnp.sum(near, axis=-1, keepdims=True) + jnp.sum(far, axis=-1, keepdims=True)
            tops[slot, k] = jnp.broadcast_to(top, (rows, head_size))
            sums[slot, k] = jnp.broadcast_to(total, (rows, head_size))
        for u, k in chains:
            r, b, slot = work[u]
            span = pl.ds(pl.multiple_of(b * key_block, key_block), key_block)
            parts[slot, k] = jnp.dot(
                far_probs[u, k], keys[r, 1, k, span, :], preferred_element_type=jnp.float32
            ) + jnp.dot(near_probs[u, k], win_values[k], preferred_element_type=jnp.float32)
        return carry

    lax.fori_loop(0, (items + ITEMS - 1) // ITEMS, item_step, 0)

    def combine(r, carry):
        count = used_blocks(r)
        at = pl.ds(pl.multiple_of(r * window_len, window_len), window_len)
        for k in range(kv_heads):
            top = tops[r * blocks, k]
            for b in range(1, blocks):
                top = jnp.where(b < count, jnp.maximum(top, tops[r * blocks + b, k]), top)
            total, value = 0.0, 0.0
            for b in range(blocks):
                share = jnp.exp2((tops[r * blocks + b, k] - top) * factor)
                added = sums[r * blocks + b, k] * share
                moved = parts[r * blocks + b, k] * share
                total = total + (added if b == 0 else jnp.where(b < count, added, 0.0))
                value = value + (moved if b == 0 else jnp.where(b < count, moved, 0.0))
            value = value / total
            for g in range(rows // window_len):
                start = (k * (rows // window_len) + g) * head_size
                wide[at, start : start + head_size] = value[g * window_len : (g + 1) * window_len]
        return carry

    lax.fori_loop(0, requests, combine, 0, unroll=2)
    out[...] = wide[...].astype(out.dtype)


def attend(first, requests, queries, window, cache, lengths, pages):
    _, window_len, heads, head_size = queries.shape
    kv_heads, page_tok = cache.shape[2], cache.shape[3]
    max_keys = pages.shape[1] * page_tok
    rows_all = window_len * heads
    rows = rows_all // kv_heads
    slots = requests * (max_keys // min(KEY_BLOCK, max_keys)) + 1
    flat = queries.reshape(queries.shape[0], rows_all, head_size)
    smem = pl.BlockSpec(memory_space=pltpu.SMEM)
    take = first // requests
    return pl.pallas_call(
        functools.partial(attend_kernel, first),
        grid=(1,),
        in_specs=[
            smem,
            smem,
            pl.BlockSpec((requests, rows_all, head_size), lambda i: (take, 0, 0)),
            pl.BlockSpec((requests,) + window.shape[1:], lambda i: (take, 0, 0, 0, 0)),
            pl.BlockSpec(memory_space=pl.ANY),
        ],
        out_specs=pl.BlockSpec((requests * window_len, heads * head_size), lambda i: (0, 0)),
        out_shape=pltpu.VMEM((requests * window_len, heads * head_size), jnp.bfloat16),
        scratch_shapes=[
            pltpu.VMEM((requests, 2, kv_heads, max_keys, head_size), jnp.bfloat16),
            pltpu.SemaphoreType.DMA((requests, pages.shape[1])),
            pltpu.SMEM((slots + 1,), jnp.int32),
            pltpu.SMEM((slots + 1,), jnp.int32),
            pltpu.VMEM((requests, rows_all, head_size), jnp.bfloat16),
            pltpu.VMEM((slots, kv_heads, rows, head_size), jnp.float32),
            pltpu.VMEM((slots, kv_heads, rows, head_size), jnp.float32),
            pltpu.VMEM((slots, kv_heads, rows, head_size), jnp.float32),
            pltpu.VMEM((requests * window_len, heads * head_size), jnp.float32),
            pltpu.VMEM((ITEMS, kv_heads, rows, requests * window_len), jnp.float32),
            pltpu.VMEM((ITEMS, kv_heads, rows, min(KEY_BLOCK, max_keys)), jnp.float32),
            pltpu.VMEM((ITEMS, kv_heads, rows, requests * window_len), jnp.bfloat16),
            pltpu.VMEM((ITEMS, kv_heads, rows, min(KEY_BLOCK, max_keys)), jnp.bfloat16),
        ],
        compiler_params=room(
            (requests, 2, kv_heads, max_keys, head_size),
            (10, slots, kv_heads, rows, head_size),
            (8, requests, rows_all, head_size),
        ),
        cost_estimate=pl.CostEstimate(flops=500000000, bytes_accessed=12000000, transcendentals=0),
        name="attend",
    )(lengths, pages, far(flat), far(window), far(cache))


def project_kernel(count, extra, flip, *refs):
    rows, weights, added = refs[:count], refs[count], refs[count + 1 : count + 1 + extra]
    out, stored, sems = refs[count + 1 + extra :]
    blocks, _, block = stored.shape
    start = (lax.axis_index("tp") ^ flip) * (blocks * block)

    def weight_copy(b):
        at = pl.ds(pl.multiple_of(start + b * block, block), block)
        return pltpu.make_async_copy(weights.at[:, at], stored.at[b], sems.at[b])

    for b in range(blocks):
        weight_copy(b).start()

    def step(b, carry):
        weight_copy(b).wait()
        at = pl.ds(pl.multiple_of(b * block, block), block)
        held = jnp.concatenate([r[...] for r in rows], axis=0)
        made = jnp.dot(held, stored[b], preferred_element_type=jnp.float32)
        if extra:
            made = made + added[0][:, at].astype(jnp.float32)
            made = made + jnp.concatenate([x[:, at] for x in added[1:]], axis=0).astype(jnp.float32)
        out[:, at] = made.astype(out.dtype)
        return carry

    lax.fori_loop(0, blocks, step, 0)


def project(chunks, weights, flip, pieces, added=()):
    depth, width = weights.shape
    own = width // pieces
    block = min(256, own)
    blocks = own // block
    total = sum(c.shape[0] for c in chunks)
    vmem = pl.BlockSpec(memory_space=pltpu.VMEM)
    return pl.pallas_call(
        functools.partial(project_kernel, len(chunks), len(added), flip),
        in_specs=[vmem] * len(chunks)
        + [pl.BlockSpec(memory_space=pl.ANY)]
        + [vmem] * len(added),
        out_specs=vmem,
        out_shape=pltpu.VMEM((total, own), jnp.bfloat16),
        scratch_shapes=[
            pltpu.VMEM((blocks, depth, block), jnp.bfloat16),
            pltpu.SemaphoreType.DMA((blocks,)),
        ],
        compiler_params=room((depth, own), (2, total, depth)),
        cost_estimate=pl.CostEstimate(
            flops=2 * total * depth * own,
            bytes_accessed=2 * (depth * own + total * (depth + own)),
            transcendentals=0,
        ),
        name="project",
    )(*[near(c) for c in chunks], far(weights), *[near(x) for x in added])


def pick(table, index):
    value = jnp.int32(table[0])
    for i in range(1, len(table)):
        value = jnp.where(index == i, jnp.int32(table[i]), value)
    return value


def local_slots(section, pool, adapters_of, slot_of, order, steps, first, count, pages_here):
    section, pool = section[0], pool[0]
    adapters = slot_of.shape[0] // adapters_of.shape[0]
    place_of = [order.index(p) for p in range(len(order))]
    place = pick(place_of, pool)
    slots = []
    for step in steps:
        group = pick(order, lax.rem(place - step + len(order), len(order)))
        for r in range(count):
            slot = slot_of[section * adapters + adapters_of[section, group, first + r]]
            slots.append(slot - section * adapters - pool * pages_here)
    return slots


def rank_kernel(order, first, count, section, pool, adapters_of, slot_of, down, *refs):
    held, out = refs[:-1], refs[-1]
    pages_here, rank_width, features = down.shape
    wide_cols = pages_here * rank_width
    lanes = out.shape[1]
    slots = local_slots(
        section, pool, adapters_of, slot_of, order, range(len(order)), first, count, pages_here
    )
    rows = jnp.concatenate([h[...] for h in held], axis=0)
    wide = lax.dot_general(
        rows, down[...].reshape(wide_cols, features), (((1,), (1,)), ((), ())),
        preferred_element_type=jnp.float32,
    )
    window_len = rows.shape[0] // len(slots)
    page = lax.broadcasted_iota(jnp.int32, (window_len, wide_cols), 1) // rank_width
    folded = []
    for i, slot in enumerate(slots):
        kept = jnp.where(page == slot, wide[i * window_len : (i + 1) * window_len], 0.0)
        total = kept[:, :lanes]
        for start in range(lanes, wide_cols, lanes):
            total = total + kept[:, start : start + lanes]
        folded.append(total)
    total = jnp.concatenate(folded, axis=0)
    both = total + pltpu.roll(total, rank_width, 1)
    half = both.shape[0] // 2
    lane = lax.broadcasted_iota(jnp.int32, (half, lanes), 1)
    out[...] = jnp.where(lane < rank_width, both[:half], both[half:]).astype(out.dtype)


def up_kernel(order, first, count, parts, section, pool, adapters_of, slot_of, up, *refs):
    ranks, outs = refs[:parts], refs[parts:]
    pages_here, rank_width, features = up.shape
    wide_cols = pages_here * rank_width
    each = outs[0].shape[0]
    slots = local_slots(
        section, pool, adapters_of, slot_of, order, range(len(order)), first, count, pages_here
    )
    packed = ranks[0][...].astype(jnp.float32)
    for other in ranks[1:]:
        packed = packed + other[...].astype(jnp.float32)
    lanes = packed.shape[1]
    turned = pltpu.roll(packed, rank_width, 1)
    lane = lax.broadcasted_iota(jnp.int32, packed.shape, 1)
    total = jnp.concatenate(
        [
            jnp.where(lane < rank_width, packed, turned),
            jnp.where(lane < rank_width, turned, packed),
        ],
        axis=0,
    )
    window_len = total.shape[0] // len(slots)
    page = lax.broadcasted_iota(jnp.int32, (window_len, wide_cols), 1) // rank_width
    spread = []
    for i, slot in enumerate(slots):
        block = total[i * window_len : (i + 1) * window_len]
        tiled = jnp.concatenate([block] * (wide_cols // lanes), axis=1)
        spread.append(jnp.where(page == slot, tiled, 0.0))
    spread = jnp.concatenate(spread, axis=0).astype(jnp.bfloat16)
    block = min(512, features)
    for start in range(0, features, block):
        made = jnp.dot(
            spread,
            up[:, :, start : start + block].reshape(wide_cols, block),
            preferred_element_type=jnp.float32,
        ).astype(jnp.bfloat16)
        for i, out in enumerate(outs):
            out[:, start : start + block] = made[i * each : (i + 1) * each]


def room(*shapes):
    return pltpu.CompilerParams(
        vmem_limit_bytes=(4 << 20) + sum(2 * math.prod(s) for s in shapes)
    )


def far(value):
    return pltpu.with_memory_space_constraint(value, pltpu.HBM)


def near(value):
    return pltpu.with_memory_space_constraint(value, pltpu.VMEM)


def small_call(kernel, scalars, weights, arrays, outs, flops):
    smem = pl.BlockSpec(memory_space=pltpu.SMEM)
    vmem = pl.BlockSpec(memory_space=pltpu.VMEM)
    moved = weights.size + sum(x.size for x in arrays)
    arrays = [near(x) for x in arrays]
    return pl.pallas_call(
        kernel,
        in_specs=[smem] * len(scalars) + [vmem] * (1 + len(arrays)),
        out_specs=[vmem] * len(outs),
        out_shape=[pltpu.VMEM(x.shape, x.dtype) for x in outs],
        compiler_params=room(*[(4,) + x.shape for x in arrays + outs], (2,) + weights.shape),
        cost_estimate=pl.CostEstimate(flops=flops, bytes_accessed=2 * moved, transcendentals=0),
    )(*scalars, near(weights), *arrays)


def sum_kernel(*refs):
    arrays, out = refs[:-1], refs[-1]
    value = arrays[0][...].astype(jnp.float32)
    for other in arrays[1:]:
        value = value + other[...].astype(jnp.float32)
    out[...] = value.astype(out.dtype)


def add(a, b):
    vmem = pl.BlockSpec(memory_space=pltpu.VMEM)
    return pl.pallas_call(
        sum_kernel,
        in_specs=[vmem] * 2,
        out_specs=vmem,
        out_shape=pltpu.VMEM(a.shape, a.dtype),
        compiler_params=room((4,) + a.shape),
        cost_estimate=pl.CostEstimate(flops=a.size, bytes_accessed=6 * a.size, transcendentals=0),
        name="add",
    )(near(a), near(b))


def finish_kernel(count, *refs):
    wholes, parts, out = refs[:count], refs[count:-1], refs[-1]
    each = parts[0].shape[0]
    for i, part in enumerate(parts):
        at = slice(i * each, (i + 1) * each)
        value = part[...].astype(jnp.float32)
        for other in wholes:
            value = value + other[at, :].astype(jnp.float32)
        out[at, :] = value.astype(out.dtype)


def finish(wholes, parts):
    vmem = pl.BlockSpec(memory_space=pltpu.VMEM)
    shape = wholes[0].shape
    return pl.pallas_call(
        functools.partial(finish_kernel, len(wholes)),
        in_specs=[vmem] * (len(wholes) + len(parts)),
        out_specs=vmem,
        out_shape=jax.ShapeDtypeStruct(shape, jnp.bfloat16),
        compiler_params=room((4,) + shape),
        cost_estimate=pl.CostEstimate(
            flops=5 * math.prod(shape), bytes_accessed=12 * math.prod(shape), transcendentals=0
        ),
        name="finish",
    )(*[near(x) for x in wholes], *[near(x) for x in parts])


def after(value, *earlier):
    return lax.optimization_barrier((value,) + earlier)[0]


def per_device(
    hidden,
    queries,
    window_key_value,
    cached_key_value,
    cached_length,
    request_page_table,
    request_adapter,
    layer_page_slot,
    wo,
    adapter_down,
    adapter_up,
):
    sections = lax.axis_size("section")
    pools = lax.axis_size("pool")
    splits = lax.axis_size("tp")
    groups = queries.shape[2]
    window_len = queries.shape[3]
    part = groups // CHUNKS
    part_rows = part * window_len
    pages_here, rank_width, features = adapter_down.shape
    own_width = adapter_up.shape[2]
    wide_cols = pages_here * rank_width
    scalars = (
        jnp.reshape(lax.axis_index("section"), (1,)).astype(jnp.int32),
        jnp.reshape(lax.axis_index("pool"), (1,)).astype(jnp.int32),
        request_adapter,
        layer_page_slot,
    )

    order = list(range(0, pools, 2)) + list(range(1, pools, 2))[::-1]
    ring = [(order[i], order[(i + 1) % pools]) for i in range(pools)]
    ring_next = [
        (s * pools + a, ((s + 1) % sections) * pools + b) for s in range(sections) for a, b in ring
    ]

    def attend_part(c, asked):
        return attend(
            c * part,
            part,
            asked,
            window_key_value[0, 0],
            cached_key_value[0, 0],
            cached_length[0, 0],
            request_page_table[0, 0],
        )

    def gather(value):
        return lax.ppermute(value, "pool", ring)

    offsets = list(range(1, splits)) + [0]

    def project_piece(i, earlier, added=()):
        first = after(contexts[0], *earlier)
        return project([first] + contexts[1:], wo[0], offsets[i], splits, added)

    def send_piece(i, piece):
        pairs = [
            (s * splits + t, ((s + 1) % sections) * splits + (t ^ offsets[i]))
            for s in range(sections)
            for t in range(splits)
        ]
        return lax.ppermute(piece, ("section", "tp"), pairs)

    lanes = min(2 * rank_width, wide_cols)
    rank_rows = pools * part_rows // 2

    def rank_of(c, earlier):
        arrays = [after(held[c][0], earlier)] + held[c][1:]
        return small_call(
            functools.partial(rank_kernel, order, c * part, part),
            scalars,
            adapter_down,
            arrays,
            [jax.ShapeDtypeStruct((rank_rows, lanes), jnp.bfloat16)],
            2 * pools * part_rows * wide_cols * features,
        )[0]

    def up_of(c, mine, earlier):
        ranks = [after(mine, earlier)]
        for d in range(splits - 1, 0, -1):
            pairs = [(t, t ^ d) for t in range(splits)]
            ranks.append(lax.ppermute(mine, "tp", pairs))
        return small_call(
            functools.partial(up_kernel, order, c * part, part, len(ranks)),
            scalars,
            adapter_up,
            ranks,
            [jax.ShapeDtypeStruct((part_rows, own_width), jnp.bfloat16)] * pools,
            2 * pools * part_rows * wide_cols * own_width,
        )

    def scatter(step, value):
        if step == pools - 1:
            return lax.ppermute(value, ("section", "pool"), ring_next)
        return lax.ppermute(value, "pool", ring)

    contexts = [attend_part(0, queries[0, 0])]
    contexts.append(attend_part(1, after(queries[0, 0], contexts[0])))
    held = [[c] for c in contexts]
    held[0].append(gather(contexts[0]))
    held[0].append(gather(held[0][1]))
    held[1].append(gather(contexts[1]))
    pieces = [project_piece(0, [held[0][1]])]
    arrived = [send_piece(0, pieces[0])]
    held[0].append(gather(after(held[0][2], pieces[0])))
    pieces.append(project_piece(1, [pieces[0], held[0][2]]))
    arrived.append(send_piece(1, pieces[1]))
    held[1].append(gather(after(held[1][1], pieces[1])))
    pieces.append(project_piece(2, [pieces[1], held[1][1]]))
    for _ in range(4, pools):
        held[0].append(gather(held[0][-1]))
    rank0 = rank_of(0, pieces[2])
    held[1].append(gather(after(held[1][2], rank0)))
    for _ in range(4, pools):
        held[1].append(gather(held[1][-1]))
    outs0 = up_of(0, rank0, held[1][2])
    moving0 = scatter(1, outs0[1])
    rank1 = rank_of(1, outs0[0])
    moving0 = scatter(2, add(after(moving0, rank1), outs0[2]))
    outs1 = up_of(1, rank1, rank1)
    moving1 = scatter(1, outs1[1])
    arrived.append(send_piece(2, after(pieces[2], outs1[0])))
    moving0 = scatter(3, add(after(moving0, outs1[0]), outs0[3]))
    added = add(after(moving1, outs1[0]), outs1[2])
    moving1 = scatter(2, added)
    pieces.append(project_piece(3, [pieces[2], added], [hidden[0, 0], outs0[0], outs1[0]]))
    arrived.append(send_piece(3, pieces[3]))
    moving1 = scatter(3, add(after(moving1, pieces[3]), outs1[3]))
    for step in range(4, pools):
        moving0 = scatter(step, add(moving0, outs0[step]))
        moving1 = scatter(step, add(moving1, outs1[step]))

    return finish(arrived, [moving0, moving1])[None, None]


def solution(mesh):
    return jax.shard_map(
        per_device,
        mesh=mesh,
        in_specs=(
            P("section", "pool", None, "tp"),
            P("section", "pool", None, None, "tp", None),
            P("section", "pool", None, None, "tp", None, None),
            P("section", "pool", None, None, "tp", None, None),
            P("section", "pool", None),
            P("section", "pool", None, None),
            P(),
            P(),
            P("section", "tp", None),
            P(("section", "pool"), None, "tp"),
            P(("section", "pool"), None, "tp"),
        ),
        out_specs=P("section", "pool", None, "tp"),
        check_vma=False,
    )
```

```python
import functools
import math

import jax
import jax.numpy as jnp
from jax import lax
from jax.experimental import pallas as pl
from jax.experimental.pallas import tpu as pltpu
from jax.sharding import PartitionSpec as P


CHUNKS = 2
KEY_BLOCK = 512
ITEMS = 4


def attend_kernel(first, lengths, pages, queries, window, cache, out, keys, sems, item_request, item_block, ordered, tops, sums, parts, wide, near_scores, far_scores, near_probs, far_probs):
    requests, rows_all, head_size = ordered.shape
    kv_heads = keys.shape[2]
    page_tok = cache.shape[3]
    window_len = window.shape[3]
    key_block = min(KEY_BLOCK, keys.shape[3])
    blocks = keys.shape[3] // key_block
    per_block = key_block // page_tok
    rows = rows_all // kv_heads
    heads_all = rows_all // window_len
    factor = head_size ** (-0.5) * math.log2(math.e)

    def page_copy(r, j):
        return pltpu.make_async_copy(
            cache.at[pages[first + r, j]],
            keys.at[r, :, :, pl.ds(pl.multiple_of(j * page_tok, page_tok), page_tok), :],
            sems.at[r, j],
        )

    def used_pages(r):
        return (lengths[first + r] + page_tok - 1) // page_tok

    def used_blocks(r):
        return (lengths[first + r] + key_block - 1) // key_block

    def start_request(r, items):
        count = used_pages(r)

        def one(j, c):
            page_copy(r, j).start()
            return c

        lax.fori_loop(0, count, one, 0)

        def clear(j, c):
            at = pl.ds(pl.multiple_of(j * page_tok, page_tok), page_tok)
            keys[r, 1, :, at, :] = jnp.zeros((kv_heads, page_tok, head_size), keys.dtype)
            return c

        lax.fori_loop(count, used_blocks(r) * per_block, clear, 0)

        def note(b, at):
            item_request[at] = r
            item_block[at] = b
            return at + 1

        return lax.fori_loop(0, used_blocks(r), note, items)

    items = lax.fori_loop(0, requests, start_request, 0)
    item_request[items] = 0
    item_block[items] = 0

    target = lax.broadcasted_iota(jnp.int32, (rows_all, rows_all), 0)
    source = lax.broadcasted_iota(jnp.int32, (rows_all, rows_all), 1)
    moved = (target % window_len) * heads_all + target // window_len
    permutation = jnp.where(source == moved, 1.0, 0.0).astype(jnp.bfloat16)

    def prepare(r, carry):
        ordered[r] = jnp.dot(
            permutation, queries[r], preferred_element_type=jnp.float32
        ).astype(jnp.bfloat16)
        return carry

    lax.fori_loop(0, requests, prepare, 0, unroll=4)

    last = (((1,), (1,)), ((), ()))
    win_cols = requests * window_len
    win_col = lax.broadcasted_iota(jnp.int32, (rows, win_cols), 1)
    win_row = lax.broadcasted_iota(jnp.int32, (rows, win_cols), 0)
    win_of = jnp.where((win_col % window_len) <= (win_row % window_len), win_col // window_len, -1)
    col = lax.broadcasted_iota(jnp.int32, (rows, key_block), 1)
    win_keys = []
    win_values = []
    for k in range(kv_heads):
        for store, kind in ((win_keys, 0), (win_values, 1)):
            taken = window[:, kind, k].astype(jnp.float32).reshape(win_cols, head_size)
            store.append(taken.astype(jnp.bfloat16))

    def item_step(i, carry):
        work = []
        for u in range(ITEMS):
            at = jnp.minimum(i * ITEMS + u, items)
            real = at < items
            r, b = item_request[at], item_block[at]
            stop = jnp.where(real, jnp.minimum(used_pages(r), (b + 1) * per_block), 0)

            def arrive(j, c, r=r):
                page_copy(r, j).wait()
                return c

            lax.fori_loop(b * per_block, stop, arrive, 0)
            work.append((r, b, jnp.where(real, r * blocks + b, requests * blocks)))
        chains = [(u, k) for u in range(ITEMS) for k in range(kv_heads)]
        peaks = {}
        for u, k in chains:
            r, b, slot = work[u]
            span = pl.ds(pl.multiple_of(b * key_block, key_block), key_block)
            asked = ordered[r, k * rows : (k + 1) * rows, :]
            near = lax.dot_general(asked, win_keys[k], last, preferred_element_type=jnp.float32)
            far = lax.dot_general(
                asked, keys[r, 0, k, span, :], last, preferred_element_type=jnp.float32
            )
            near = jnp.where(win_of == jnp.where(b == 0, r, requests), near, -jnp.inf)
            far = jnp.where(col < lengths[first + r] - b * key_block, far, -jnp.inf)
            near_scores[u, k] = near
            far_scores[u, k] = far
            peaks[u, k] = jnp.maximum(
                jnp.max(near, axis=-1, keepdims=True), jnp.max(far, axis=-1, keepdims=True)
            )
        for u, k in chains:
            slot = work[u][2]
            top = peaks[u, k]
            near = jnp.exp2((near_scores[u, k] - top) * factor)
            far = jnp.exp2((far_scores[u, k] - top) * factor)
            near_probs[u, k] = near.astype(jnp.bfloat16)
            far_probs[u, k] = far.astype(jnp.bfloat16)
            total = jnp.sum(near, axis=-1, keepdims=True) + jnp.sum(far, axis=-1, keepdims=True)
            tops[slot, k] = jnp.broadcast_to(top, (rows, head_size))
            sums[slot, k] = jnp.broadcast_to(total, (rows, head_size))
        for u, k in chains:
            r, b, slot = work[u]
            span = pl.ds(pl.multiple_of(b * key_block, key_block), key_block)
            parts[slot, k] = jnp.dot(
                far_probs[u, k], keys[r, 1, k, span, :], preferred_element_type=jnp.float32
            ) + jnp.dot(near_probs[u, k], win_values[k], preferred_element_type=jnp.float32)
        return carry

    lax.fori_loop(0, (items + ITEMS - 1) // ITEMS, item_step, 0)

    def combine(r, carry):
        count = used_blocks(r)
        at = pl.ds(pl.multiple_of(r * window_len, window_len), window_len)
        for k in range(kv_heads):
            top = tops[r * blocks, k]
            for b in range(1, blocks):
                top = jnp.where(b < count, jnp.maximum(top, tops[r * blocks + b, k]), top)
            total, value = 0.0, 0.0
            for b in range(blocks):
                share = jnp.exp2((tops[r * blocks + b, k] - top) * factor)
                added = sums[r * blocks + b, k] * share
                moved = parts[r * blocks + b, k] * share
                total = total + (added if b == 0 else jnp.where(b < count, added, 0.0))
                value = value + (moved if b == 0 else jnp.where(b < count, moved, 0.0))
            value = value / total
            for g in range(rows // window_len):
                start = (k * (rows // window_len) + g) * head_size
                wide[at, start : start + head_size] = value[g * window_len : (g + 1) * window_len]
        return carry

    lax.fori_loop(0, requests, combine, 0, unroll=2)
    out[...] = wide[...].astype(out.dtype)


def attend(first, requests, queries, window, cache, lengths, pages):
    _, window_len, heads, head_size = queries.shape
    kv_heads, page_tok = cache.shape[2], cache.shape[3]
    max_keys = pages.shape[1] * page_tok
    rows_all = window_len * heads
    rows = rows_all // kv_heads
    slots = requests * (max_keys // min(KEY_BLOCK, max_keys)) + 1
    flat = queries.reshape(queries.shape[0], rows_all, head_size)
    smem = pl.BlockSpec(memory_space=pltpu.SMEM)
    take = first // requests
    return pl.pallas_call(
        functools.partial(attend_kernel, first),
        grid=(1,),
        in_specs=[
            smem,
            smem,
            pl.BlockSpec((requests, rows_all, head_size), lambda i: (take, 0, 0)),
            pl.BlockSpec((requests,) + window.shape[1:], lambda i: (take, 0, 0, 0, 0)),
            pl.BlockSpec(memory_space=pl.ANY),
        ],
        out_specs=pl.BlockSpec((requests * window_len, heads * head_size), lambda i: (0, 0)),
        out_shape=pltpu.VMEM((requests * window_len, heads * head_size), jnp.bfloat16),
        scratch_shapes=[
            pltpu.VMEM((requests, 2, kv_heads, max_keys, head_size), jnp.bfloat16),
            pltpu.SemaphoreType.DMA((requests, pages.shape[1])),
            pltpu.SMEM((slots + 1,), jnp.int32),
            pltpu.SMEM((slots + 1,), jnp.int32),
            pltpu.VMEM((requests, rows_all, head_size), jnp.bfloat16),
            pltpu.VMEM((slots, kv_heads, rows, head_size), jnp.float32),
            pltpu.VMEM((slots, kv_heads, rows, head_size), jnp.float32),
            pltpu.VMEM((slots, kv_heads, rows, head_size), jnp.float32),
            pltpu.VMEM((requests * window_len, heads * head_size), jnp.float32),
            pltpu.VMEM((ITEMS, kv_heads, rows, requests * window_len), jnp.float32),
            pltpu.VMEM((ITEMS, kv_heads, rows, min(KEY_BLOCK, max_keys)), jnp.float32),
            pltpu.VMEM((ITEMS, kv_heads, rows, requests * window_len), jnp.bfloat16),
            pltpu.VMEM((ITEMS, kv_heads, rows, min(KEY_BLOCK, max_keys)), jnp.bfloat16),
        ],
        compiler_params=room(
            (requests, 2, kv_heads, max_keys, head_size),
            (10, slots, kv_heads, rows, head_size),
            (8, requests, rows_all, head_size),
        ),
        cost_estimate=pl.CostEstimate(flops=500000000, bytes_accessed=12000000, transcendentals=0),
        name="attend",
    )(far(lengths), far(pages), far(flat), far(window), far(cache))


def project_kernel(count, extra, flip, *refs):
    rows, weights, added = refs[:count], refs[count], refs[count + 1 : count + 1 + extra]
    out, stored, sems = refs[count + 1 + extra :]
    blocks, _, block = stored.shape
    start = (lax.axis_index("tp") ^ flip) * (blocks * block)

    def weight_copy(b):
        at = pl.ds(pl.multiple_of(start + b * block, block), block)
        return pltpu.make_async_copy(weights.at[:, at], stored.at[b], sems.at[b])

    for b in range(blocks):
        weight_copy(b).start()

    def step(b, carry):
        weight_copy(b).wait()
        at = pl.ds(pl.multiple_of(b * block, block), block)
        held = jnp.concatenate([r[...] for r in rows], axis=0)
        made = jnp.dot(held, stored[b], preferred_element_type=jnp.float32)
        if extra:
            made = made + added[0][:, at].astype(jnp.float32)
            made = made + jnp.concatenate([x[:, at] for x in added[1:]], axis=0).astype(jnp.float32)
        out[:, at] = made.astype(out.dtype)
        return carry

    lax.fori_loop(0, blocks, step, 0)


def project(chunks, weights, flip, pieces, added=()):
    depth, width = weights.shape
    own = width // pieces
    block = min(256, own)
    blocks = own // block
    total = sum(c.shape[0] for c in chunks)
    vmem = pl.BlockSpec(memory_space=pltpu.VMEM)
    return pl.pallas_call(
        functools.partial(project_kernel, len(chunks), len(added), flip),
        in_specs=[vmem] * len(chunks)
        + [pl.BlockSpec(memory_space=pl.ANY)]
        + [vmem] * len(added),
        out_specs=vmem,
        out_shape=pltpu.VMEM((total, own), jnp.bfloat16),
        scratch_shapes=[
            pltpu.VMEM((blocks, depth, block), jnp.bfloat16),
            pltpu.SemaphoreType.DMA((blocks,)),
        ],
        compiler_params=room((depth, own), (2, total, depth)),
        cost_estimate=pl.CostEstimate(
            flops=2 * total * depth * own,
            bytes_accessed=2 * (depth * own + total * (depth + own)),
            transcendentals=0,
        ),
        name="project",
    )(*[near(c) for c in chunks], far(weights), *[near(x) for x in added])


def local_slots(section, pool, adapters_of, slot_of, first, count, pages_here):
    section, pool = section[0], pool[0]
    sections, pools, _ = adapters_of.shape
    adapters = slot_of.shape[0] // sections
    slots = []
    for step in range(pools):
        for r in range(count):
            slot = slot_of[section * adapters + adapters_of[section, pool ^ step, first + r]]
            slots.append(slot - section * adapters - pool * pages_here)
    return slots


def is_inner(pools):
    pool = lax.axis_index("pool")
    return (pool > 0) & (pool < pools - 1)


def rank_kernel(first, count, section, pool, adapters_of, slot_of, down, *refs):
    held, out = refs[:-1], refs[-1]
    pools = adapters_of.shape[1]
    pages_here, rank_width, features = down.shape
    wide_cols = pages_here * rank_width
    lanes = out.shape[1]
    slots = local_slots(section, pool, adapters_of, slot_of, first, count, pages_here)
    taken = [h[...] for h in held[:pools]]
    if len(held) > pools:
        taken[-1] = jnp.where(is_inner(pools), taken[-1], held[pools][...])
    rows = jnp.concatenate(taken, axis=0)
    wide = lax.dot_general(
        rows, down[...].reshape(wide_cols, features), (((1,), (1,)), ((), ())),
        preferred_element_type=jnp.float32,
    )
    window_len = rows.shape[0] // len(slots)
    page = lax.broadcasted_iota(jnp.int32, (window_len, wide_cols), 1) // rank_width
    folded = []
    for i, slot in enumerate(slots):
        kept = jnp.where(page == slot, wide[i * window_len : (i + 1) * window_len], 0.0)
        total = kept[:, :lanes]
        for start in range(lanes, wide_cols, lanes):
            total = total + kept[:, start : start + lanes]
        folded.append(total)
    total = jnp.concatenate(folded, axis=0)
    both = total + pltpu.roll(total, rank_width, 1)
    half = both.shape[0] // 2
    lane = lax.broadcasted_iota(jnp.int32, (half, lanes), 1)
    out[...] = jnp.where(lane < rank_width, both[:half], both[half:]).astype(out.dtype)


def up_kernel(first, count, parts, section, pool, adapters_of, slot_of, up, *refs):
    ranks, outs = refs[:parts], refs[parts:]
    pages_here, rank_width, features = up.shape
    wide_cols = pages_here * rank_width
    each = outs[0].shape[0]
    slots = local_slots(section, pool, adapters_of, slot_of, first, count, pages_here)
    packed = ranks[0][...].astype(jnp.float32)
    for other in ranks[1:]:
        packed = packed + other[...].astype(jnp.float32)
    lanes = packed.shape[1]
    turned = pltpu.roll(packed, rank_width, 1)
    lane = lax.broadcasted_iota(jnp.int32, packed.shape, 1)
    total = jnp.concatenate(
        [
            jnp.where(lane < rank_width, packed, turned),
            jnp.where(lane < rank_width, turned, packed),
        ],
        axis=0,
    )
    window_len = total.shape[0] // len(slots)
    page = lax.broadcasted_iota(jnp.int32, (window_len, wide_cols), 1) // rank_width
    spread = []
    for i, slot in enumerate(slots):
        block = total[i * window_len : (i + 1) * window_len]
        tiled = jnp.concatenate([block] * (wide_cols // lanes), axis=1)
        spread.append(jnp.where(page == slot, tiled, 0.0))
    spread = jnp.concatenate(spread, axis=0).astype(jnp.bfloat16)
    block = min(512, features)
    for start in range(0, features, block):
        made = jnp.dot(
            spread,
            up[:, :, start : start + block].reshape(wide_cols, block),
            preferred_element_type=jnp.float32,
        ).astype(jnp.bfloat16)
        for i, out in enumerate(outs):
            out[:, start : start + block] = made[i * each : (i + 1) * each]


def room(*shapes):
    return pltpu.CompilerParams(
        vmem_limit_bytes=(4 << 20) + sum(2 * math.prod(s) for s in shapes)
    )


def far(value):
    return pltpu.with_memory_space_constraint(value, pltpu.HBM)


def near(value):
    return pltpu.with_memory_space_constraint(value, pltpu.VMEM)


def small_call(kernel, scalars, weights, arrays, outs, flops):
    smem = pl.BlockSpec(memory_space=pltpu.SMEM)
    vmem = pl.BlockSpec(memory_space=pltpu.VMEM)
    moved = weights.size + sum(x.size for x in arrays)
    arrays = [near(x) for x in arrays]
    return pl.pallas_call(
        kernel,
        in_specs=[smem] * len(scalars) + [vmem] * (1 + len(arrays)),
        out_specs=[vmem] * len(outs),
        out_shape=[pltpu.VMEM(x.shape, x.dtype) for x in outs],
        compiler_params=room(*[(4,) + x.shape for x in arrays + outs], (2,) + weights.shape),
        cost_estimate=pl.CostEstimate(flops=flops, bytes_accessed=2 * moved, transcendentals=0),
    )(*scalars, near(weights), *arrays)


def join_kernel(pools, a, b, out):
    out[...] = jnp.where(is_inner(pools), a[...] + b[...], a[...])


def join(pools, a, b):
    vmem = pl.BlockSpec(memory_space=pltpu.VMEM)
    return pl.pallas_call(
        functools.partial(join_kernel, pools),
        in_specs=[vmem] * 2,
        out_specs=vmem,
        out_shape=pltpu.VMEM(a.shape, a.dtype),
        compiler_params=room((4,) + a.shape),
        cost_estimate=pl.CostEstimate(flops=a.size, bytes_accessed=6 * a.size, transcendentals=0),
        name="join",
    )(near(a), near(b))


def finish_kernel(count, each, pools, relayed, *refs):
    wholes, parts, out = refs[:count], refs[count:-1], refs[-1]
    chunks = len(parts) // each
    rows = parts[0].shape[0]
    for i in range(chunks):
        at = slice(i * rows, (i + 1) * rows)
        value = 0.0
        for j in range(each):
            term = parts[i * each + j][...].astype(jnp.float32)
            if relayed and j == each - 1:
                term = jnp.where(is_inner(pools), term, 0.0)
            value = value + term
        for other in wholes:
            value = value + other[at, :].astype(jnp.float32)
        out[at, :] = value.astype(out.dtype)


def finish(pools, relayed, wholes, parts):
    vmem = pl.BlockSpec(memory_space=pltpu.VMEM)
    shape = wholes[0].shape
    flat = [x for group in parts for x in group]
    return pl.pallas_call(
        functools.partial(finish_kernel, len(wholes), len(parts[0]), pools, relayed),
        in_specs=[vmem] * (len(wholes) + len(flat)),
        out_specs=vmem,
        out_shape=jax.ShapeDtypeStruct(shape, jnp.bfloat16),
        compiler_params=room((4,) + shape),
        cost_estimate=pl.CostEstimate(
            flops=5 * math.prod(shape), bytes_accessed=12 * math.prod(shape), transcendentals=0
        ),
        name="finish",
    )(*[near(x) for x in wholes], *[near(x) for x in flat])


def after(value, *earlier):
    return lax.optimization_barrier((value,) + earlier)[0]


def per_device(
    hidden,
    queries,
    window_key_value,
    cached_key_value,
    cached_length,
    request_page_table,
    request_adapter,
    layer_page_slot,
    wo,
    adapter_down,
    adapter_up,
):
    sections = lax.axis_size("section")
    pools = lax.axis_size("pool")
    splits = lax.axis_size("tp")
    groups = queries.shape[2]
    window_len = queries.shape[3]
    part = groups // CHUNKS
    part_rows = part * window_len
    pages_here, rank_width, features = adapter_down.shape
    own_width = adapter_up.shape[2]
    wide_cols = pages_here * rank_width
    scalars = (
        jnp.reshape(lax.axis_index("section"), (1,)).astype(jnp.int32),
        jnp.reshape(lax.axis_index("pool"), (1,)).astype(jnp.int32),
        request_adapter,
        layer_page_slot,
    )

    relayed = pools == 4
    middle = [(0, 0), (1, 2), (2, 1), (3, 3)]
    far_step = 2 if relayed else 1

    def swap(step):
        return [(p, p ^ step) for p in range(pools)]

    def onward(pairs):
        return [
            (s * pools + a, ((s + 1) % sections) * pools + b)
            for s in range(sections)
            for a, b in pairs
        ]

    def attend_part(c, asked):
        return attend(
            c * part,
            part,
            asked,
            window_key_value[0, 0],
            cached_key_value[0, 0],
            cached_length[0, 0],
            request_page_table[0, 0],
        )

    def gather(c, step):
        pairs = middle if relayed and step == 3 else swap(step)
        return lax.ppermute(contexts[c], "pool", pairs)

    def relay(c, *earlier):
        if relayed:
            value = after(held[c][2], *earlier)
            held[c].append(lax.ppermute(value, "pool", swap(1)))

    def scatter(outs):
        back = lax.ppermute(outs[3], "pool", swap(1)) if relayed else None
        got = {}
        for step in range(1, pools):
            if not (relayed and step == 2):
                pairs = middle if relayed and step == 3 else swap(step)
                got[step] = lax.ppermute(outs[step], ("section", "pool"), onward(pairs))
        return back, got

    def scatter_far(outs, back, got, earlier):
        if not relayed:
            return earlier
        joined = join(pools, outs[2], after(back, earlier))
        got[2] = lax.ppermute(joined, ("section", "pool"), onward(swap(2)))
        return joined

    offsets = list(range(splits - 1, 0, -1)) + [0]

    def project_piece(i, earlier, added=()):
        first = after(contexts[0], *earlier)
        return project([first] + contexts[1:], wo[0], offsets[i], splits, added)

    def send_piece(i, piece):
        pairs = [
            (s * splits + t, ((s + 1) % sections) * splits + (t ^ offsets[i]))
            for s in range(sections)
            for t in range(splits)
        ]
        return lax.ppermute(piece, ("section", "tp"), pairs)

    lanes = min(2 * rank_width, wide_cols)
    rank_rows = pools * part_rows // 2

    def rank_of(c, earlier):
        arrays = [after(held[c][0], earlier)] + held[c][1:]
        return small_call(
            functools.partial(rank_kernel, c * part, part),
            scalars,
            adapter_down,
            arrays,
            [jax.ShapeDtypeStruct((rank_rows, lanes), jnp.bfloat16)],
            2 * pools * part_rows * wide_cols * features,
        )[0]

    def up_of(c, mine, earlier):
        ranks = [after(mine, earlier)]
        for d in range(splits - 1, 0, -1):
            pairs = [(t, t ^ d) for t in range(splits)]
            ranks.append(lax.ppermute(mine, "tp", pairs))
        return small_call(
            functools.partial(up_kernel, c * part, part, len(ranks)),
            scalars,
            adapter_up,
            ranks,
            [jax.ShapeDtypeStruct((part_rows, own_width), jnp.bfloat16)] * pools,
            2 * pools * part_rows * wide_cols * own_width,
        )

    contexts = [attend_part(0, queries[0, 0])]
    contexts.append(attend_part(1, after(queries[0, 0], contexts[0])))
    held = []
    for c in range(CHUNKS):
        held.append([contexts[c]] + [gather(c, step) for step in range(1, pools)])
    relay(0)
    pieces = [project_piece(0, [contexts[1], held[0][far_step]])]
    rank0 = rank_of(0, pieces[0])
    relay(1, rank0)
    arrived = [send_piece(0, after(pieces[0], rank0))]
    pieces.append(project_piece(1, [pieces[0], rank0, held[1][far_step]]))
    outs0 = up_of(0, rank0, pieces[1])
    back0, got0 = scatter(outs0)
    rank1 = rank_of(1, outs0[0])
    joined0 = scatter_far(outs0, back0, got0, rank1)
    outs1 = up_of(1, rank1, joined0)
    back1, got1 = scatter(outs1)
    arrived.append(send_piece(1, after(pieces[1], outs1[0])))
    pieces.append(project_piece(2, [pieces[1], outs1[0]]))
    joined1 = scatter_far(outs1, back1, got1, pieces[2])
    arrived.append(send_piece(2, pieces[2]))
    pieces.append(
        project_piece(3, [pieces[2], joined1], [hidden[0, 0], outs0[0], outs1[0]])
    )
    arrived.append(send_piece(3, pieces[3]))
    parts = [[got[step] for step in range(1, pools)] for got in (got0, got1)]
    return finish(pools, relayed, arrived, parts)[None, None]


def solution(mesh):
    return jax.shard_map(
        per_device,
        mesh=mesh,
        in_specs=(
            P("section", "pool", None, "tp"),
            P("section", "pool", None, None, "tp", None),
            P("section", "pool", None, None, "tp", None, None),
            P("section", "pool", None, None, "tp", None, None),
            P("section", "pool", None),
            P("section", "pool", None, None),
            P(),
            P(),
            P("section", "tp", None),
            P(("section", "pool"), None, "tp"),
            P(("section", "pool"), None, "tp"),
        ),
        out_specs=P("section", "pool", None, "tp"),
        check_vma=False,
    )
```
